32 devices in a mesh: patch: 2 (over x), epoch: 16 (over z, y, core).
Axes of the slice: x: 2, y: 2, z: 4, core: 2. Of those that a mesh axis runs over, the one named last changes fastest.
Arguments:
- epoch_images: float32 [32, 64, 4096], P(('patch', 'epoch')), parts along dimension 0, may hold values from -8 to 8
- mask_words: int32 [32, 1, 128], P(('patch', 'epoch')), parts along dimension 0, may hold values from -2147483648 to 2147483647, as said below
- coefficients: float32 [32, 49, 3], P('patch'), parts along dimension 0, may hold values from -2 to 2
- epoch_order: int32 [32], P('patch'), parts along dimension 0, may hold values from 0 to 15, each once
Outputs:
- difference: float32 [32, 32, 4096], P(('patch', 'epoch')), parts along dimension 0
The draws below stay inside these ranges and needn't reach their ends.
There are 2 independent parts, one for each index of `patch`. The reference program is written for one: setup_inputs(seed, part) draws one part's arguments, and reference() takes and returns one part's arrays. A program takes and returns all parts, laid end to end along the dimension named above; each array names one. Nothing has to cross between parts.
Inputs may be any that keep to these rules, and one draw needn't show every extreme that they name: `mask_words`: bit b of word w in band n of an epoch marks column 32 w + b of rows n * 64 to (n + 1) * 64 - 1 of that epoch valid (1) or masked (0), bit 31 being the sign bit; some cells are masked in every epoch. A permutation: image slot e uses the coefficients of catalog epoch epoch_order[e].
All inputs are finite; a program needn't handle non-finite values.
Results may differ from the reference program's by a relative error of at most 0.000057.
Values sent between devices are 32-bit elements; how exact they have to be, the bound alone decides.
No kernel may reach another device: no remote copies, remote signals or barrier semaphores. Data moves between devices by JAX's collectives and lax.ppermute only.
A program may use at most 64 MiB of HBM per device.

```python
import math
import jax
import jax.numpy as jnp
from jax import lax

W = 4096
ROWS = 32
HALF = 15
MARGIN = 16
BAND = 64
KERNELS = 49
POLY = 3
EPOCHS = 16


def draw_epoch_images(key, part):
    sky_key = jax.random.fold_in(key, 101)
    noise_key = jax.random.fold_in(key, 202)
    padded_rows = ROWS + 2 * MARGIN
    sky_field = jax.random.normal(sky_key, (padded_rows, W), jnp.float32)
    noise_field = jax.random.normal(noise_key, (EPOCHS, padded_rows, W), jnp.float32)
    return jnp.clip(sky_field[None] + noise_field, -8.0, 8.0)


def draw_mask_words(key, part):
    bands = (ROWS + 2 * MARGIN) // BAND
    common = jax.random.randint(jax.random.fold_in(key, 11), (bands, W), 0, 64) == 0
    epoch_good = jax.random.randint(jax.random.fold_in(key, 12), (EPOCHS, bands, W), 0, 8) != 0
    good_bits = jnp.logical_and(epoch_good, jnp.logical_not(common[None])).astype(jnp.int32)
    good_bits = good_bits.reshape(EPOCHS, bands, W // 32, 32)
    placed = jnp.left_shift(good_bits, jnp.arange(32, dtype=jnp.int32))
    return jnp.sum(placed, axis=-1, dtype=jnp.int32)


def scatter_about(rng, dims, deviation, limit, held_as=jnp.bfloat16):
    drawn = jax.random.normal(rng, dims, jnp.float32) * deviation
    return jnp.minimum(jnp.maximum(drawn, -limit), limit).astype(held_as)


def setup_inputs(seed: int = 0, part: int = 0) -> dict:
    arg_keys = jax.random.split(jax.random.key(seed), 5)
    part_keys = jax.random.split(jax.random.fold_in(arg_keys[4], part), 5)
    epoch_images = draw_epoch_images(jax.random.fold_in(jax.random.fold_in(arg_keys[4], part), 71), part)
    mask_words = draw_mask_words(jax.random.fold_in(jax.random.fold_in(arg_keys[4], part), 71), part)
    coefficients = scatter_about(part_keys[2], (EPOCHS, KERNELS, POLY), 0.3, 2.0, jnp.float32)
    epoch_order = jax.random.permutation(part_keys[3], EPOCHS).astype(jnp.int32)
    return dict(epoch_images=epoch_images, mask_words=mask_words, coefficients=coefficients, epoch_order=epoch_order)


gauss_widths = (1.5, 3.0, 6.0)
gauss_degrees = (6, 4, 2)

def basis_filters(half_width):
    offsets = jnp.arange(-half_width, half_width + 1).astype(jnp.float32)
    result = []
    for spread_width, degree in zip(gauss_widths, gauss_degrees):
        envelope = jnp.exp(-offsets * offsets / (2.0 * spread_width * spread_width)) / (math.sqrt(2.0 * math.pi) * spread_width)
        for vert_power in range(degree + 1):
            result.append(envelope * (offsets / spread_width) ** vert_power)
    return jnp.stack(result)

def kernel_pairs():
    result = []
    first_index = 0
    for degree in gauss_degrees:
        for vert_power in range(degree + 1):
            for horiz_power in range(degree + 1 - vert_power):
                result.append((first_index + vert_power, first_index + horiz_power))
        first_index = first_index + degree + 1
    return result

def unpack_valid(mask_words):
    bit_places = jnp.arange(32, dtype=jnp.int32)
    bit_values = jnp.right_shift(mask_words[..., None], bit_places) & 1
    word_shape = mask_words.shape
    return bit_values.reshape(word_shape[0], word_shape[1], word_shape[2] * 32).astype(jnp.float32)

def reference(epoch_images, mask_words, coefficients, epoch_order):
    band_valid = unpack_valid(mask_words)
    valid_mask = jnp.repeat(band_valid, BAND, axis=1)
    masked_sum = lax.optimization_barrier(jnp.sum(valid_mask * epoch_images, axis=0))
    counts = jnp.repeat(lax.optimization_barrier(jnp.sum(band_valid, axis=0)), BAND, axis=0)
    template = masked_sum / jnp.maximum(counts, 1.0)
    filters = basis_filters(HALF)
    tap_count = 2 * HALF + 1
    vertical = []
    for filter_index in range(filters.shape[0]):
        running = jnp.zeros((ROWS, W), jnp.float32)
        for offset in range(tap_count):
            start_row = MARGIN - HALF + offset
            running = running + filters[filter_index, offset] * template[start_row:start_row + ROWS]
        vertical.append(running)
    vertical = jnp.stack(vertical)
    padded = jnp.pad(vertical, ((0, 0), (0, 0), (HALF, HALF)))
    convolved = []
    for vert_index, horiz_index in kernel_pairs():
        running = jnp.zeros((ROWS, W), jnp.float32)
        for offset in range(tap_count):
            running = running + filters[horiz_index, offset] * padded[vert_index, :, offset:offset + W]
        convolved.append(running)
    convolved = jnp.stack(convolved)
    columns = (2.0 * jnp.arange(W).astype(jnp.float32) + 1.0) / W - 1.0
    row_pos = (2.0 * jnp.arange(ROWS).astype(jnp.float32) + 1.0) / ROWS - 1.0
    spatial = jnp.stack([jnp.ones((ROWS, W), jnp.float32), jnp.broadcast_to(columns[None, :], (ROWS, W)), jnp.broadcast_to(row_pos[:, None], (ROWS, W))])
    basis_images = (convolved[:, None] * spatial[None]).reshape(KERNELS * POLY, ROWS * W)
    coef_table = coefficients[epoch_order].reshape(EPOCHS, KERNELS * POLY)
    model_image = jnp.dot(coef_table, basis_images, precision=lax.Precision.HIGHEST, preferred_element_type=jnp.float32).reshape(EPOCHS, ROWS, W)
    centre = epoch_images[:, MARGIN:MARGIN + ROWS]
    return valid_mask[:, MARGIN:MARGIN + ROWS] * (centre - model_image)
```

```python
import functools
import math

import jax
import jax.numpy as jnp
import numpy as np
from jax import lax
from jax.experimental import pallas as pl
from jax.experimental.pallas import tpu as pltpu
from jax.sharding import PartitionSpec as P

HALF = 15
MARGIN = 16
BAND = 64
LANES = 128
SHIFTS = 4
GROUPS = 8

gauss_widths = (1.5, 3.0, 6.0)
gauss_degrees = (6, 4, 2)


def basis_filters():
    offsets = np.arange(-HALF, HALF + 1).astype(np.float64)
    result = []
    for width, degree in zip(gauss_widths, gauss_degrees):
        envelope = np.exp(-offsets * offsets / (2.0 * width * width)) / (math.sqrt(2.0 * math.pi) * width)
        for power in range(degree + 1):
            result.append(envelope * (offsets / width) ** power)
    return np.stack(result)


def kernel_pairs():
    result = []
    first_index = 0
    for degree in gauss_degrees:
        for vert_power in range(degree + 1):
            for horiz_power in range(degree + 1 - vert_power):
                result.append((first_index + vert_power, first_index + horiz_power))
        first_index = first_index + degree + 1
    return result


def tables(rows, padded_rows):
    filters = basis_filters()
    count, taps = filters.shape
    pairs = kernel_pairs()
    vert_pick = np.zeros((len(pairs), count + 1), np.float32)
    horiz_pick = np.zeros((len(pairs), count + 1), np.float32)
    for index, (vert, horiz) in enumerate(pairs):
        vert_pick[index, vert] = 1.0
        horiz_pick[index, horiz] = 1.0
    span = SHIFTS * GROUPS
    horiz = np.zeros((count + 1, span), np.float64)
    horiz[:count, :taps] = filters
    horiz_lanes = np.repeat(horiz, padded_rows, axis=1).astype(np.float32)
    vert = np.zeros((count, rows, padded_rows), np.float64)
    for row in range(rows):
        start = row + MARGIN - HALF
        vert[:, row, start : start + taps] = filters
    vert_lanes = np.tile(vert, (1, 1, SHIFTS)).astype(np.float32)
    return vert_pick, horiz_pick, horiz_lanes, vert_lanes


def valid_lanes(words, first_column, columns):
    word_count = words.shape[1]
    byte_row = lax.broadcasted_iota(jnp.int32, (8, word_count), 0)
    octets = jnp.right_shift(jnp.broadcast_to(words, (8, word_count)), 8 * (byte_row & 3)) & 255
    octets = octets.astype(jnp.float32).astype(jnp.bfloat16)
    word_row = lax.broadcasted_iota(jnp.int32, (word_count, columns), 0)
    word_col = jnp.right_shift(lax.broadcasted_iota(jnp.int32, (word_count, columns), 1) + first_column, 5)
    spread = jnp.where(word_row == word_col, 1.0, 0.0).astype(jnp.bfloat16)
    wide = jnp.dot(octets, spread, preferred_element_type=jnp.float32).astype(jnp.int32)
    lane = lax.broadcasted_iota(jnp.int32, (8, columns), 1)
    row = lax.broadcasted_iota(jnp.int32, (8, columns), 0)
    bit = jnp.right_shift(wide, lane & 7) & 1
    bit = jnp.where(row == (jnp.right_shift(lane, 3) & 3), bit, 0).astype(jnp.float32)
    return jnp.sum(bit, axis=0, keepdims=True)


def mask_kernel(words_ref, image_ref, masked_ref, valid_ref):
    columns = image_ref.shape[1]
    valid = valid_lanes(words_ref[...], pl.program_id(0) * columns, columns)
    valid_ref[...] = valid
    row = lax.broadcasted_iota(jnp.int32, image_ref.shape, 0)
    masked_ref[...] = jnp.where(row == 0, valid, valid * image_ref[...])


def masked_image(words, image, blocks):
    rows, columns = image.shape
    width = columns // blocks
    return pl.pallas_call(
        mask_kernel,
        grid=(blocks,),
        in_specs=[
            pl.BlockSpec(words.shape, lambda i: (0, 0)),
            pl.BlockSpec((rows, width), lambda i: (0, i)),
        ],
        out_specs=[
            pl.BlockSpec((rows, width), lambda i: (0, i)),
            pl.BlockSpec((1, width), lambda i: (0, i)),
        ],
        out_shape=[
            jax.ShapeDtypeStruct((rows, columns), jnp.float32),
            jax.ShapeDtypeStruct((1, columns), jnp.float32),
        ],
        name="mask_image",
    )(words, image)


def weight_kernel(place_ref, order_ref, coef_ref, vert_pick_ref, horiz_pick_ref, horiz_ref, vert_ref, high_ref, low_ref):
    count, rows, lanes = vert_ref.shape
    coef = coef_ref[0]
    terms = []
    for term in range(3):
        table = lax.dot_general(
            vert_pick_ref[...] * coef[:, term : term + 1],
            horiz_pick_ref[...],
            (((0,), (0,)), ((), ())),
            precision=lax.Precision.HIGHEST,
            preferred_element_type=jnp.float32,
        )
        terms.append(
            jnp.dot(table, horiz_ref[...], precision=lax.Precision.HIGHEST, preferred_element_type=jnp.float32)
        )
    row = lax.broadcasted_iota(jnp.int32, (rows, lanes), 0).astype(jnp.float32)
    row_pos = (2.0 * row + 1.0) / rows - 1.0
    for group in range(GROUPS):
        sums = []
        for term in range(3):
            total = jnp.zeros((rows, lanes), jnp.float32)
            for index in range(count):
                taps = terms[term][index : index + 1, group * lanes : (group + 1) * lanes]
                total = total + taps * vert_ref[index]
            sums.append(total)
        for place, weight in enumerate((sums[0] + row_pos * sums[2], sums[1])):
            high = weight.astype(jnp.bfloat16)
            low = (weight - high.astype(jnp.float32)).astype(jnp.bfloat16)
            first = (2 * group + place) * rows
            high_ref[first : first + rows] = high
            low_ref[first : first + rows] = low


def weights(coefficients, epoch_order, slot, rows, padded_rows):
    vert_pick, horiz_pick, horiz_lanes, vert_lanes = tables(rows, padded_rows)
    kernels, poly = coefficients.shape[1:]
    shape = (2 * GROUPS * rows, SHIFTS * padded_rows)
    whole = lambda array: pl.BlockSpec(array.shape, lambda i, place, order: (0,) * array.ndim)
    return pl.pallas_call(
        weight_kernel,
        grid_spec=pltpu.PrefetchScalarGridSpec(
            num_scalar_prefetch=2,
            grid=(1,),
            in_specs=[
                pl.BlockSpec((1, kernels, poly), lambda i, place, order: (order[place[0]], 0, 0)),
                whole(vert_pick),
                whole(horiz_pick),
                whole(horiz_lanes),
                whole(vert_lanes),
            ],
            out_specs=[pl.BlockSpec(shape, lambda i, place, order: (0, 0))] * 2,
        ),
        out_shape=[jax.ShapeDtypeStruct(shape, jnp.bfloat16)] * 2,
        name="kernel_weights",
    )(slot, epoch_order, coefficients, vert_pick, horiz_pick, horiz_lanes, vert_lanes)


def difference_kernel(
    high_ref, low_ref, template_ref, image_ref, valid_ref, out_ref, wide_high, wide_low, partial
):
    padded_rows, columns = template_ref.shape
    rows = out_ref.shape[0]
    domain = wide_high.shape[1]
    template = jnp.concatenate(
        [template_ref[...], jnp.zeros((padded_rows, domain - columns), jnp.float32)], axis=1
    )
    for shift in range(SHIFTS):
        moved = template if shift == 0 else pltpu.roll(template, domain - shift, 1)
        high = moved.astype(jnp.bfloat16)
        low = (moved - high.astype(jnp.float32)).astype(jnp.bfloat16)
        wide_high[shift * padded_rows : (shift + 1) * padded_rows] = high
        wide_low[shift * padded_rows : (shift + 1) * padded_rows] = low

    tile = 384

    def product(index, carry):
        lanes = pl.ds(pl.multiple_of(index * tile, tile), tile)
        high = wide_high[:, lanes]
        total = jnp.dot(high_ref[...], high, preferred_element_type=jnp.float32)
        total += jnp.dot(low_ref[...], high, preferred_element_type=jnp.float32)
        total += jnp.dot(high_ref[...], wide_low[:, lanes], preferred_element_type=jnp.float32)
        partial[:, lanes] = total
        return carry

    lax.fori_loop(0, domain // tile, product, 0)
    size = 2 * rows
    total = jnp.zeros((size, domain), jnp.float32)
    for group in range(GROUPS):
        amount = (HALF - SHIFTS * group) % domain
        total = total + pltpu.roll(partial[group * size : (group + 1) * size], amount, 1)
    column = lax.broadcasted_iota(jnp.int32, (rows, columns), 1).astype(jnp.float32)
    column = (2.0 * column + 1.0) / columns - 1.0
    model = total[:rows, :columns] + column * total[rows:, :columns]
    out_ref[...] = valid_ref[...] * (image_ref[...] - model)


def difference(high, low, template, centre, valid):
    padded_rows, columns = template.shape
    rows = centre.shape[0]
    domain = columns + LANES
    vmem = pl.BlockSpec(memory_space=pltpu.VMEM)
    return pl.pallas_call(
        difference_kernel,
        in_specs=[vmem] * 5,
        out_specs=vmem,
        out_shape=jax.ShapeDtypeStruct((rows, columns), jnp.float32),
        scratch_shapes=[
            pltpu.VMEM((SHIFTS * padded_rows, domain), jnp.bfloat16),
            pltpu.VMEM((SHIFTS * padded_rows, domain), jnp.bfloat16),
            pltpu.VMEM((2 * GROUPS * rows, domain), jnp.float32),
        ],
        name="difference",
    )(high, low, template, centre, valid)


def exchange(cells, bit):
    count = lax.axis_size("epoch")
    return lax.ppermute(cells, "epoch", [(i, i ^ (1 << bit)) for i in range(count)])


def shards(epoch_images, mask_words, coefficients, epoch_order):
    padded_rows, columns = epoch_images.shape[1:]
    rows = padded_rows - 2 * MARGIN
    place = lax.axis_index("epoch")
    bits = lax.axis_size("epoch").bit_length() - 1
    image = epoch_images[0]
    cells, valid = masked_image(mask_words[0], image, 2)
    high, low = weights(coefficients, epoch_order, place[None].astype(jnp.int32), rows, padded_rows)
    for bit in range(bits):
        width = cells.shape[1] // 2
        side = jnp.right_shift(place, bit) & 1
        keep = lax.dynamic_slice_in_dim(cells, side * width, width, 1)
        send = lax.dynamic_slice_in_dim(cells, (1 - side) * width, width, 1)
        cells = keep + exchange(send, bit)
    cells = cells / jnp.maximum(cells[:1], 1.0)
    for bit in reversed(range(bits)):
        other = exchange(cells, bit)
        side = jnp.right_shift(place, bit) & 1
        cells = jnp.where(
            side == 0, jnp.concatenate([cells, other], axis=1), jnp.concatenate([other, cells], axis=1)
        )
    centre = image[MARGIN : MARGIN + rows]
    return difference(high, low, cells, centre, valid)[None]


def solution(mesh):
    placed = (
        P(("patch", "epoch"), None, None),
        P(("patch", "epoch"), None, None),
        P("patch", None, None),
        P("patch"),
    )
    return jax.shard_map(
        shards,
        mesh=mesh,
        in_specs=placed,
        out_specs=P(("patch", "epoch"), None, None),
        check_vma=False,
    )
```

```python
import math

import jax
import jax.numpy as jnp
import numpy as np
from jax import lax
from jax.experimental import pallas as pl
from jax.experimental.pallas import tpu as pltpu
from jax.sharding import PartitionSpec as P

HALF = 15
MARGIN = 16
BAND = 64
LANES = 128
SHIFTS = 8
GROUPS = 4
GRANT = 20 << 20

gauss_widths = (1.5, 3.0, 6.0)
gauss_degrees = (6, 4, 2)


def basis_filters():
    offsets = np.arange(-HALF, HALF + 1).astype(np.float64)
    result = []
    for width, degree in zip(gauss_widths, gauss_degrees):
        envelope = np.exp(-offsets * offsets / (2.0 * width * width)) / (math.sqrt(2.0 * math.pi) * width)
        for power in range(degree + 1):
            result.append(envelope * (offsets / width) ** power)
    return np.stack(result)


def kernel_pairs():
    result = []
    first_index = 0
    for degree in gauss_degrees:
        for vert_power in range(degree + 1):
            for horiz_power in range(degree + 1 - vert_power):
                result.append((first_index + vert_power, first_index + horiz_power))
        first_index = first_index + degree + 1
    return result


def tables(rows, padded_rows):
    filters = basis_filters()
    count, taps = filters.shape
    pairs = kernel_pairs()
    vert_pick = np.zeros((count + 1, len(pairs)), np.float32)
    horiz_pick = np.zeros((len(pairs), count + 1), np.float32)
    for index, (vert, horiz) in enumerate(pairs):
        vert_pick[vert, index] = 1.0
        horiz_pick[index, horiz] = 1.0
    span = SHIFTS * GROUPS
    horiz = np.zeros((count + 1, span), np.float64)
    horiz[:count, :taps] = filters
    horiz_lanes = np.repeat(horiz, padded_rows, axis=1).astype(np.float32)
    vert = np.zeros((count, rows, padded_rows), np.float64)
    for row in range(rows):
        start = row + MARGIN - HALF
        vert[:, row, start : start + taps] = filters
    vert_lanes = np.tile(vert, (1, 1, SHIFTS)).astype(np.float32)
    return vert_pick, horiz_pick, horiz_lanes, vert_lanes


def valid_lanes(words, first_column, columns):
    word_count = words.shape[1]
    byte_row = lax.broadcasted_iota(jnp.int32, (8, word_count), 0)
    octets = jnp.right_shift(jnp.broadcast_to(words, (8, word_count)), 8 * (byte_row & 3)) & 255
    octets = octets.astype(jnp.float32).astype(jnp.bfloat16)
    word_row = lax.broadcasted_iota(jnp.int32, (word_count, columns), 0)
    word_col = jnp.right_shift(lax.broadcasted_iota(jnp.int32, (word_count, columns), 1) + first_column, 5)
    spread = jnp.where(word_row == word_col, 1.0, 0.0).astype(jnp.bfloat16)
    wide = jnp.dot(octets, spread, preferred_element_type=jnp.float32).astype(jnp.int32)
    lane = lax.broadcasted_iota(jnp.int32, (8, columns), 1)
    row = lax.broadcasted_iota(jnp.int32, (8, columns), 0)
    bit = jnp.right_shift(wide, lane & 7) & 1
    bit = jnp.where(row == (jnp.right_shift(lane, 3) & 3), bit, 0).astype(jnp.float32)
    return jnp.sum(bit, axis=0, keepdims=True)


def mask_kernel(side_ref, words_ref, image_ref, masked_ref, valid_ref):
    columns = image_ref.shape[1]
    valid = valid_lanes(words_ref[...], side_ref[0] * columns, columns)
    valid_ref[...] = valid
    row = lax.broadcasted_iota(jnp.int32, image_ref.shape, 0)
    masked_ref[...] = jnp.where(row == 0, valid, valid * image_ref[...])


def masked_half(side, words, image):
    rows, columns = image.shape
    half = columns // 2
    return pl.pallas_call(
        mask_kernel,
        grid_spec=pltpu.PrefetchScalarGridSpec(
            num_scalar_prefetch=1,
            grid=(1,),
            in_specs=[
                pl.BlockSpec(words.shape, lambda i, side: (0, 0)),
                pl.BlockSpec((rows, half), lambda i, side: (0, side[0])),
            ],
            out_specs=[
                pl.BlockSpec((rows, half), lambda i, side: (0, 0)),
                pl.BlockSpec((1, half), lambda i, side: (0, 0)),
            ],
        ),
        out_shape=[
            jax.ShapeDtypeStruct((rows, half), jnp.float32),
            jax.ShapeDtypeStruct((1, half), jnp.float32),
        ],
        compiler_params=pltpu.CompilerParams(vmem_limit_bytes=GRANT),
        cost_estimate=pl.CostEstimate(flops=rows * half, bytes_accessed=8 * rows * half, transcendentals=0),
        name="mask_half",
    )(side[None], words, image)


def weight_kernel(place_ref, order_ref, coef_ref, vert_pick_ref, horiz_pick_ref, horiz_ref, vert_ref, high_ref, low_ref):
    count, rows, lanes = vert_ref.shape
    exact = dict(precision=lax.Precision.HIGHEST, preferred_element_type=jnp.float32)
    catalog = order_ref[place_ref[0]]
    picked = [vert_pick_ref[...] * coef_ref[term, pl.ds(catalog, 1), :] for term in range(3)]
    table = jnp.dot(jnp.concatenate(picked, axis=0), horiz_pick_ref[...], **exact)
    taps = jnp.dot(table, horiz_ref[...], **exact)
    step = count + 1
    row = lax.broadcasted_iota(jnp.int32, (rows, lanes), 0).astype(jnp.float32)
    row_pos = (2.0 * row + 1.0) / rows - 1.0
    for group in range(GROUPS):
        sums = []
        for term in range(3):
            total = jnp.zeros((rows, lanes), jnp.float32)
            for index in range(count):
                line = term * step + index
                total = total + taps[line : line + 1, group * lanes : (group + 1) * lanes] * vert_ref[index]
            sums.append(total)
        for place, weight in enumerate((sums[0] + row_pos * sums[2], sums[1])):
            high = weight.astype(jnp.bfloat16)
            low = (weight - high.astype(jnp.float32)).astype(jnp.bfloat16)
            first = (2 * group + place) * rows
            high_ref[first : first + rows] = high
            low_ref[first : first + rows] = low


def weights(coefficients, epoch_order, slot, rows, padded_rows):
    arrays = (jnp.transpose(coefficients, (2, 0, 1)),) + tables(rows, padded_rows)
    shape = (2 * GROUPS * rows, SHIFTS * padded_rows)
    smem = pl.BlockSpec(memory_space=pltpu.SMEM)
    vmem = pl.BlockSpec(memory_space=pltpu.VMEM)
    return pl.pallas_call(
        weight_kernel,
        in_specs=[smem, smem] + [vmem] * len(arrays),
        out_specs=[vmem, vmem],
        out_shape=[jax.ShapeDtypeStruct(shape, jnp.bfloat16)] * 2,
        compiler_params=pltpu.CompilerParams(vmem_limit_bytes=GRANT),
        cost_estimate=pl.CostEstimate(flops=10**8, bytes_accessed=2 * 10**6, transcendentals=0),
        name="kernel_weights",
    )(slot[None], epoch_order, *arrays)


def half_model(high_ref, low_ref, template_ref, first_column, total_columns, wide_high, wide_low, partial):
    padded_rows, columns = template_ref.shape
    domain = wide_high.shape[1]
    size = partial.shape[0] // GROUPS
    rows = size // 2
    template = jnp.concatenate(
        [template_ref[...], jnp.zeros((padded_rows, domain - columns), jnp.float32)], axis=1
    )
    for shift in range(SHIFTS):
        moved = template if shift == 0 else pltpu.roll(template, domain - shift, 1)
        high = moved.astype(jnp.bfloat16)
        low = (moved - high.astype(jnp.float32)).astype(jnp.bfloat16)
        wide_high[shift * padded_rows : (shift + 1) * padded_rows] = high
        wide_low[shift * padded_rows : (shift + 1) * padded_rows] = low
    for lanes in (slice(0, columns // 2), slice(columns // 2, domain)):
        high = wide_high[:, lanes]
        total = jnp.dot(high_ref[...], high, preferred_element_type=jnp.float32)
        total += jnp.dot(low_ref[...], high, preferred_element_type=jnp.float32)
        total += jnp.dot(high_ref[...], wide_low[:, lanes], preferred_element_type=jnp.float32)
        partial[:, lanes] = total
    total = jnp.zeros((size, domain), jnp.float32)
    for group in range(GROUPS):
        amount = (HALF - SHIFTS * group) % domain
        total = total + pltpu.roll(partial[group * size : (group + 1) * size], amount, 1)
    lane = lax.broadcasted_iota(jnp.int32, (rows, domain), 1)
    column = first_column + jnp.where(lane < columns + LANES // 2, lane, lane - domain)
    position = (2.0 * column.astype(jnp.float32) + 1.0) / total_columns - 1.0
    return total[:rows] + position * total[rows:]


def near_kernel(side_ref, high_ref, low_ref, template_ref, model_ref, wide_high, wide_low, partial):
    half = template_ref.shape[1]
    model_ref[...] = half_model(
        high_ref, low_ref, template_ref, side_ref[0] * half, 2 * half, wide_high, wide_low, partial
    )


def far_kernel(
    side_ref, high_ref, low_ref, template_ref, near_ref, image_ref, near_valid_ref, far_valid_ref, out_ref,
    wide_high, wide_low, partial,
):
    half = template_ref.shape[1]
    rows = out_ref.shape[0]
    side = side_ref[0]
    far = half_model(
        high_ref, low_ref, template_ref, (1 - side) * half, 2 * half, wide_high, wide_low, partial
    )
    near = near_ref[...]
    lane = lax.broadcasted_iota(jnp.int32, (rows, LANES), 1)
    centre = slice(MARGIN, MARGIN + rows)
    for model, other, valid_ref, place in ((near, far, near_valid_ref, side), (far, near, far_valid_ref, 1 - side)):
        spill = other[:, half:]
        left = jnp.where((place == 1) & (lane < LANES // 2), spill, 0.0)
        right = jnp.where((place == 0) & (lane >= LANES // 2), spill, 0.0)
        whole = jnp.concatenate(
            [model[:, :LANES] + left, model[:, LANES : half - LANES], model[:, half - LANES : half] + right], axis=1
        )
        lanes = pl.ds(pl.multiple_of(place * half, half), half)
        out_ref[:, lanes] = valid_ref[...] * (image_ref[centre, lanes] - whole)


def model_scratch(rows, padded_rows, half):
    domain = half + LANES
    return [
        pltpu.VMEM((SHIFTS * padded_rows, domain), jnp.bfloat16),
        pltpu.VMEM((SHIFTS * padded_rows, domain), jnp.bfloat16),
        pltpu.VMEM((2 * GROUPS * rows, domain), jnp.float32),
    ]


def model_cost(rows, padded_rows, half):
    flops = 12 * GROUPS * rows * SHIFTS * padded_rows * (half + LANES)
    return pl.CostEstimate(flops=flops, bytes_accessed=10 * padded_rows * half, transcendentals=0)


def near_model(side, high, low, template, rows):
    padded_rows, half = template.shape
    vmem = pl.BlockSpec(memory_space=pltpu.VMEM)
    return pl.pallas_call(
        near_kernel,
        in_specs=[pl.BlockSpec(memory_space=pltpu.SMEM)] + [vmem] * 3,
        out_specs=vmem,
        out_shape=jax.ShapeDtypeStruct((rows, half + LANES), jnp.float32),
        scratch_shapes=model_scratch(rows, padded_rows, half),
        compiler_params=pltpu.CompilerParams(vmem_limit_bytes=GRANT),
        cost_estimate=model_cost(rows, padded_rows, half),
        name="near_model",
    )(side[None], high, low, template)


def difference(side, high, low, template, near, image, near_valid, far_valid):
    padded_rows, half = template.shape
    rows = near.shape[0]
    vmem = pl.BlockSpec(memory_space=pltpu.VMEM)
    return pl.pallas_call(
        far_kernel,
        in_specs=[pl.BlockSpec(memory_space=pltpu.SMEM)] + [vmem] * 7,
        out_specs=vmem,
        out_shape=jax.ShapeDtypeStruct((rows, 2 * half), jnp.float32),
        scratch_shapes=model_scratch(rows, padded_rows, half),
        compiler_params=pltpu.CompilerParams(vmem_limit_bytes=GRANT),
        cost_estimate=model_cost(rows, padded_rows, half),
        name="difference",
    )(side[None], high, low, template, near, image, near_valid, far_valid)


def exchange(cells, bit):
    count = lax.axis_size("epoch")
    return lax.ppermute(cells, "epoch", [(i, i ^ (1 << bit)) for i in range(count)])


def halves(cells, side):
    width = cells.shape[1] // 2
    keep = lax.dynamic_slice_in_dim(cells, side * width, width, 1)
    send = lax.dynamic_slice_in_dim(cells, (1 - side) * width, width, 1)
    return keep, send


def shards(epoch_images, mask_words, coefficients, epoch_order):
    padded_rows, columns = epoch_images.shape[1:]
    rows = padded_rows - 2 * MARGIN
    place = lax.axis_index("epoch").astype(jnp.int32)
    bits = lax.axis_size("epoch").bit_length() - 1
    sides = [jnp.right_shift(place, bit) & 1 for bit in range(bits)]
    image, words = epoch_images[0], mask_words[0]

    send, far_valid = masked_half(1 - sides[0], words, image)
    other = exchange(send, 0)
    keep, near_valid = masked_half(sides[0], words, image)
    cells = keep + other
    keep, send = halves(cells, sides[1])
    other = exchange(send, 1)
    high, low = weights(coefficients, epoch_order, place, rows, padded_rows)
    cells = keep + other
    cells, high, low = lax.optimization_barrier((cells, high, low))
    for bit in range(2, bits - 1):
        keep, send = halves(cells, sides[bit])
        cells = keep + exchange(send, bit)
    cells = cells + exchange(cells, bits - 1)
    cells = cells / jnp.maximum(cells[:1], 1.0)
    for bit in reversed(range(1, bits - 1)):
        other = exchange(cells, bit)
        cells = jnp.where(
            sides[bit] == 0, jnp.concatenate([cells, other], axis=1), jnp.concatenate([other, cells], axis=1)
        )
    other = exchange(cells, 0)
    near = near_model(sides[0], high, low, cells, rows)
    return difference(sides[0], high, low, other, near, image, near_valid, far_valid)[None]


def solution(mesh):
    placed = (
        P(("patch", "epoch"), None, None),
        P(("patch", "epoch"), None, None),
        P("patch", None, None),
        P("patch"),
    )
    return jax.shard_map(
        shards,
        mesh=mesh,
        in_specs=placed,
        out_specs=P(("patch", "epoch"), None, None),
        check_vma=False,
    )
```

```python
import functools
import math

import jax
import jax.numpy as jnp
import numpy as np
from jax import lax
from jax.experimental import pallas as pl
from jax.experimental.pallas import tpu as pltpu
from jax.sharding import PartitionSpec as P

HALF = 15
MARGIN = 16
LANES = 128
SHIFTS = 8
GROUPS = 4
GRANT = 12 << 20
STREAMS = 2

gauss_widths = (1.5, 3.0, 6.0)
gauss_degrees = (6, 4, 2)


def basis_filters():
    offsets = np.arange(-HALF, HALF + 1).astype(np.float64)
    result = []
    for width, degree in zip(gauss_widths, gauss_degrees):
        envelope = np.exp(-offsets * offsets / (2.0 * width * width)) / (math.sqrt(2.0 * math.pi) * width)
        for power in range(degree + 1):
            result.append(envelope * (offsets / width) ** power)
    return np.stack(result)


def kernel_pairs():
    result = []
    first_index = 0
    for degree in gauss_degrees:
        for vert_power in range(degree + 1):
            for horiz_power in range(degree + 1 - vert_power):
                result.append((first_index + vert_power, first_index + horiz_power))
        first_index = first_index + degree + 1
    return result


def tables(rows, padded_rows):
    filters = basis_filters()
    count, taps = filters.shape
    pairs = kernel_pairs()
    vert_pick = np.zeros((count + 1, len(pairs)), np.float32)
    horiz_pick = np.zeros((len(pairs), count + 1), np.float32)
    for index, (vert, horiz) in enumerate(pairs):
        vert_pick[vert, index] = 1.0
        horiz_pick[index, horiz] = 1.0
    span = SHIFTS * GROUPS
    horiz = np.zeros((count + 1, span), np.float64)
    horiz[:count, :taps] = filters
    horiz_lanes = np.repeat(horiz, padded_rows, axis=1).astype(np.float32)
    vert = np.zeros((count, rows, padded_rows), np.float64)
    for row in range(rows):
        start = row + MARGIN - HALF
        vert[:, row, start : start + taps] = filters
    vert_lanes = np.tile(vert, (1, 1, LANES // padded_rows)).astype(np.float32)
    return vert_pick, horiz_pick, horiz_lanes, vert_lanes


def mask_kernel(twin, stream, place_ref, octets_ref, image_ref, masked_ref, valid_ref):
    width = masked_ref.shape[1]
    word_count, piece_words = octets_ref.shape[1], width // 32
    piece = ((place_ref[0] & 1) ^ twin) * STREAMS + stream
    word_row = lax.broadcasted_iota(jnp.int32, (piece_words, width), 0)
    lane = lax.broadcasted_iota(jnp.int32, (piece_words, width), 1)
    spread = jnp.where(word_row == jnp.right_shift(lane, 5), 1.0, 0.0).astype(jnp.bfloat16)
    octets = pltpu.roll(octets_ref[...], lax.rem(word_count - piece * piece_words, word_count), 1)
    octets = octets[:, :piece_words].astype(jnp.bfloat16)
    wide = jnp.dot(octets, spread, preferred_element_type=jnp.float32).astype(jnp.int32)
    lane = lax.broadcasted_iota(jnp.int32, wide.shape, 1)
    byte_row = lax.broadcasted_iota(jnp.int32, wide.shape, 0)
    bit = jnp.right_shift(wide, lane & 7) & 1
    bit = jnp.where(byte_row == (jnp.right_shift(lane, 3) & 3), bit, 0).astype(jnp.float32)
    valid = jnp.sum(bit, axis=0, keepdims=True)
    valid_ref[...] = valid
    row = lax.broadcasted_iota(jnp.int32, masked_ref.shape, 0)
    cells = image_ref[:, pl.ds(pl.multiple_of(piece * width, width), width)]
    masked_ref[...] = jnp.where(row == 0, valid, valid * cells)


def masked_piece(place, octets, image, twin, stream):
    rows, columns = image.shape
    width = columns // (2 * STREAMS)
    vmem = pl.BlockSpec(memory_space=pltpu.VMEM)
    return pl.pallas_call(
        functools.partial(mask_kernel, twin, stream),
        in_specs=[pl.BlockSpec(memory_space=pltpu.SMEM), vmem, vmem],
        out_specs=[vmem, vmem],
        out_shape=[
            jax.ShapeDtypeStruct((rows, width), jnp.float32),
            jax.ShapeDtypeStruct((1, width), jnp.float32),
        ],
        compiler_params=pltpu.CompilerParams(vmem_limit_bytes=GRANT),
        cost_estimate=pl.CostEstimate(flops=rows * width, bytes_accessed=8 * rows * width, transcendentals=0),
        name="mask_piece",
    )(place, octets, image)


def part_kernel(bit, place_ref, kept_ref, arrived_ref, keep_ref, send_ref):
    width = keep_ref.shape[1]
    side = jnp.right_shift(place_ref[0], bit) & 1
    for target_ref, part in ((keep_ref, side), (send_ref, 1 - side)):
        lanes = pl.ds(pl.multiple_of(part * width, width), width)
        target_ref[...] = kept_ref[:, lanes] + arrived_ref[:, lanes]


def add_and_part(place, bit, kept, arrived):
    rows, width = kept.shape
    if width % (2 * LANES):
        return halves(kept + arrived, jnp.right_shift(place[0], bit) & 1)
    vmem = pl.BlockSpec(memory_space=pltpu.VMEM)
    return pl.pallas_call(
        functools.partial(part_kernel, bit),
        in_specs=[pl.BlockSpec(memory_space=pltpu.SMEM), vmem, vmem],
        out_specs=[vmem, vmem],
        out_shape=[jax.ShapeDtypeStruct((rows, width // 2), jnp.float32)] * 2,
        compiler_params=pltpu.CompilerParams(vmem_limit_bytes=GRANT),
        cost_estimate=pl.CostEstimate(flops=rows * width, bytes_accessed=12 * rows * width, transcendentals=0),
        name="add_and_part",
    )(place, kept, arrived)


def weight_kernel(place_ref, order_ref, coef_ref, vert_pick_ref, horiz_pick_ref, horiz_ref, vert_ref, high_ref, low_ref):
    count, rows, lanes = vert_ref.shape
    exact = dict(precision=lax.Precision.HIGHEST, preferred_element_type=jnp.float32)
    order = order_ref[...]
    slot = lax.broadcasted_iota(jnp.int32, order.shape, 1)
    catalog = jnp.sum(jnp.where(slot == place_ref[0], order, 0), axis=1, keepdims=True)
    chosen = lax.broadcasted_iota(jnp.int32, coef_ref.shape[1:], 0) == catalog
    picked = [
        vert_pick_ref[...] * jnp.sum(jnp.where(chosen, coef_ref[term], 0.0), axis=0, keepdims=True)
        for term in range(3)
    ]
    table = jnp.dot(jnp.concatenate(picked, axis=0), horiz_pick_ref[...], **exact)
    taps = jnp.dot(table, horiz_ref[...], **exact)
    step = count + 1
    row = lax.broadcasted_iota(jnp.int32, (rows, lanes), 0).astype(jnp.float32)
    row_pos = (2.0 * row + 1.0) / rows - 1.0
    width = high_ref.shape[1]
    for group in range(GROUPS):
        for start in range(0, width, lanes):
            sums = []
            for term in range(3):
                total = jnp.zeros((rows, lanes), jnp.float32)
                for index in range(count):
                    line = term * step + index
                    first = group * width + start
                    total = total + taps[line : line + 1, first : first + lanes] * vert_ref[index]
                sums.append(total)
            for place, weight in enumerate((sums[0] + row_pos * sums[2], sums[1])):
                high = weight.astype(jnp.bfloat16)
                low = (weight - high.astype(jnp.float32)).astype(jnp.bfloat16)
                first = (2 * group + place) * rows
                high_ref[first : first + rows, start : start + lanes] = high
                low_ref[first : first + rows, start : start + lanes] = low


def weights(place, coefficients, epoch_order, rows, padded_rows):
    arrays = (epoch_order[None], jnp.transpose(coefficients, (2, 0, 1)),) + tables(rows, padded_rows)
    shape = (2 * GROUPS * rows, SHIFTS * padded_rows)
    smem = pl.BlockSpec(memory_space=pltpu.SMEM)
    vmem = pl.BlockSpec(memory_space=pltpu.VMEM)
    return pl.pallas_call(
        weight_kernel,
        in_specs=[smem] + [vmem] * len(arrays),
        out_specs=[vmem, vmem],
        out_shape=[jax.ShapeDtypeStruct(shape, jnp.bfloat16)] * 2,
        compiler_params=pltpu.CompilerParams(vmem_limit_bytes=GRANT),
        cost_estimate=pl.CostEstimate(flops=10**8, bytes_accessed=2 * 10**6, transcendentals=0),
        name="kernel_weights",
    )(place, *arrays)


def piece_model(high_ref, low_ref, template_ref, first_column, total_columns, wide_high, wide_low, partial):
    padded_rows, columns = template_ref.shape
    domain = wide_high.shape[1]
    size = partial.shape[0] // GROUPS
    rows = size // 2
    template = jnp.concatenate(
        [template_ref[...], jnp.zeros((padded_rows, domain - columns), jnp.float32)], axis=1
    )
    for shift in range(SHIFTS):
        moved = template if shift == 0 else pltpu.roll(template, domain - shift, 1)
        high = moved.astype(jnp.bfloat16)
        low = (moved - high.astype(jnp.float32)).astype(jnp.bfloat16)
        wide_high[shift * padded_rows : (shift + 1) * padded_rows] = high
        wide_low[shift * padded_rows : (shift + 1) * padded_rows] = low
    high = wide_high[...]
    total = jnp.dot(high_ref[...], high, preferred_element_type=jnp.float32)
    total += jnp.dot(low_ref[...], high, preferred_element_type=jnp.float32)
    total += jnp.dot(high_ref[...], wide_low[...], preferred_element_type=jnp.float32)
    partial[...] = total
    total = jnp.zeros((size, domain), jnp.float32)
    for group in range(GROUPS):
        amount = (HALF - SHIFTS * group) % domain
        total = total + pltpu.roll(partial[group * size : (group + 1) * size], amount, 1)
    lane = lax.broadcasted_iota(jnp.int32, (rows, domain), 1)
    column = first_column + jnp.where(lane < columns + LANES // 2, lane, lane - domain)
    position = (2.0 * column.astype(jnp.float32) + 1.0) / total_columns - 1.0
    return total[:rows] + position * total[rows:]


def piece_column(place, bit, stream, other, twin, width):
    side = (place & 1) ^ twin
    part = (jnp.right_shift(place, bit) & 1) ^ other
    return pl.multiple_of(side * (2 * STREAMS * width) + stream * (2 * width) + part * width, LANES)


def add_pieces(pieces, place, high_ref, low_ref, template_refs, total_columns, model_ref, scratch):
    lane = lax.broadcasted_iota(jnp.int32, (model_ref.shape[0], LANES), 1)
    for index, (piece, template_ref) in enumerate(zip(pieces, template_refs)):
        width = template_ref.shape[1]
        first = piece_column(place, *piece, width)
        model = piece_model(
            high_ref, low_ref, template_ref, first, total_columns, *scratch[3 * index : 3 * index + 3]
        )
        spill = model[:, width:]
        body = pl.ds(first + LANES, width)
        model_ref[:, body] = model_ref[:, body] + model[:, :width]
        before = pl.ds(first, LANES)
        model_ref[:, before] = model_ref[:, before] + jnp.where(lane < LANES // 2, 0.0, spill)
        after = pl.ds(pl.multiple_of(first + (LANES + width), LANES), LANES)
        model_ref[:, after] = model_ref[:, after] + jnp.where(lane < LANES // 2, spill, 0.0)


def model_kernel(pieces, total_columns, fresh, place_ref, high_ref, low_ref, *refs):
    count = len(pieces)
    templates, refs = refs[:count], refs[count:]
    if fresh:
        model_ref, scratch = refs[0], refs[1:]
        model_ref[...] = jnp.zeros_like(model_ref)
    else:
        model_ref, scratch = refs[1], refs[2:]
    add_pieces(pieces, place_ref[0], high_ref, low_ref, templates, total_columns, model_ref, scratch)


def difference_kernel(pieces, place_ref, high_ref, low_ref, *refs):
    count, parts = len(pieces), 2 * STREAMS
    templates, refs = refs[:count], refs[count:]
    model_ref, image_ref, valid_refs = refs[0], refs[1], refs[2 : 2 + parts]
    out_ref, total_ref = refs[2 + parts : 4 + parts]
    rows, columns = out_ref.shape
    width = columns // parts
    total_ref[...] = model_ref[...]
    add_pieces(pieces, place_ref[0], high_ref, low_ref, templates, columns, total_ref, refs[4 + parts :])
    for part, valid_ref in enumerate(valid_refs):
        side = (place_ref[0] & 1) ^ (part // STREAMS)
        first = pl.multiple_of((side * STREAMS + part % STREAMS) * width, width)
        lanes = pl.ds(first, width)
        model = total_ref[:, pl.ds(pl.multiple_of(first + LANES, LANES), width)]
        out_ref[:, lanes] = valid_ref[...] * (image_ref[MARGIN : MARGIN + rows, lanes] - model)


def model_scratch(rows, padded_rows, width):
    domain = width + LANES
    return [
        pltpu.VMEM((SHIFTS * padded_rows, domain), jnp.bfloat16),
        pltpu.VMEM((SHIFTS * padded_rows, domain), jnp.bfloat16),
        pltpu.VMEM((2 * GROUPS * rows, domain), jnp.float32),
    ]


def model_cost(rows, padded_rows, width, pieces=1):
    flops = 12 * GROUPS * rows * SHIFTS * padded_rows * (width + LANES) * pieces
    return pl.CostEstimate(flops=flops, bytes_accessed=10 * padded_rows * width * pieces, transcendentals=0)


def add_models(place, high, low, pieces, templates, model, rows, total_columns):
    padded_rows, width = templates[0].shape
    count = len(templates)
    fresh = model is None
    vmem = pl.BlockSpec(memory_space=pltpu.VMEM)
    return pl.pallas_call(
        functools.partial(model_kernel, pieces, total_columns, fresh),
        in_specs=[pl.BlockSpec(memory_space=pltpu.SMEM)] + [vmem] * (2 + count + (not fresh)),
        out_specs=vmem,
        out_shape=jax.ShapeDtypeStruct((rows, total_columns + 2 * LANES), jnp.float32),
        scratch_shapes=model_scratch(rows, padded_rows, width) * count,
        input_output_aliases={} if fresh else {3 + count: 0},
        compiler_params=pltpu.CompilerParams(vmem_limit_bytes=GRANT),
        cost_estimate=model_cost(rows, padded_rows, width, count),
        name="add_models",
    )(place, high, low, *templates, *(() if fresh else (model,)))


def difference(place, high, low, pieces, templates, model, image, valids):
    padded_rows, width = templates[0].shape
    count = len(templates)
    rows = model.shape[0]
    vmem = pl.BlockSpec(memory_space=pltpu.VMEM)
    return pl.pallas_call(
        functools.partial(difference_kernel, pieces),
        in_specs=[pl.BlockSpec(memory_space=pltpu.SMEM)] + [vmem] * (4 + count + len(valids)),
        out_specs=vmem,
        out_shape=jax.ShapeDtypeStruct((rows, image.shape[1]), jnp.float32),
        scratch_shapes=[pltpu.VMEM(model.shape, jnp.float32)] + model_scratch(rows, padded_rows, width) * count,
        compiler_params=pltpu.CompilerParams(vmem_limit_bytes=GRANT),
        cost_estimate=model_cost(rows, padded_rows, width, count),
        name="difference",
    )(place, high, low, *templates, model, image, *valids)


def exchange(cells, bit):
    count = lax.axis_size("epoch")
    return lax.ppermute(cells, "epoch", [(i, i ^ (1 << bit)) for i in range(count)])


def halves(cells, side):
    width = cells.shape[1] // 2
    keep = lax.dynamic_slice_in_dim(cells, side * width, width, 1)
    send = lax.dynamic_slice_in_dim(cells, (1 - side) * width, width, 1)
    return keep, send


def joined_columns(cells, other, side):
    return jnp.where(side == 0, jnp.concatenate([cells, other], axis=1), jnp.concatenate([other, cells], axis=1))


def part_of_epoch(epoch_images, mask_words, coefficients, epoch_order):
    padded_rows, columns = epoch_images.shape[1:]
    rows = padded_rows - 2 * MARGIN
    index = lax.axis_index("epoch").astype(jnp.int32)
    place = index[None]
    bits = lax.axis_size("epoch").bit_length() - 1
    image, words = epoch_images[0], mask_words[0]
    orders = list(range(1, bits - 1)), [2, 1] + list(range(3, bits - 1))
    streams = range(STREAMS)

    places = 8 * (lax.broadcasted_iota(jnp.int32, (8, words.shape[1]), 0) & 3)
    octets = (jnp.right_shift(jnp.broadcast_to(words, places.shape), places) & 255).astype(jnp.float32)
    far, near = [], []
    for stream in streams:
        far.append(masked_piece(place, octets, image, 1, stream))
    others = [exchange(far[stream][0], 0) for stream in streams]
    for stream in streams:
        near.append(masked_piece(place, octets, image, 0, stream))
    cells = [near[stream][0] for stream in streams]
    for step in range(bits - 2):
        pairs = [add_and_part(place, orders[stream][step], cells[stream], others[stream]) for stream in streams]
        cells = [pairs[stream][0] for stream in streams]
        others = [exchange(pairs[stream][1], orders[stream][step]) for stream in streams]
    cells = [cells[stream] + others[stream] for stream in streams]
    others = [exchange(cells[stream], bits - 1) for stream in streams]
    high, low = weights(place, coefficients, epoch_order, rows, padded_rows)
    cells = [cells[stream] + others[stream] for stream in streams]
    cells = [part / jnp.maximum(part[:1], 1.0) for part in cells]
    for step in reversed(range(1, bits - 2)):
        others = [exchange(cells[stream], orders[stream][step]) for stream in streams]
        cells = [
            joined_columns(
                cells[stream], others[stream], jnp.right_shift(index, orders[stream][step]) & 1
            )
            for stream in streams
        ]
    kinds = [
        [(orders[stream][0], stream, other, twin) for stream in streams] for other in range(2) for twin in range(2)
    ]
    others = [exchange(cells[stream], orders[stream][0]) for stream in streams]
    twins = [exchange(cells[stream], 0) for stream in streams]
    model = None
    for stream in reversed(streams):
        model = add_models(place, high, low, [kinds[0][stream]], [cells[stream]], model, rows, columns)
    model = add_models(place, high, low, kinds[1], twins, model, rows, columns)
    twins = [exchange(others[stream], 0) for stream in streams]
    model = add_models(place, high, low, kinds[2], others, model, rows, columns)
    valids = [piece[1] for piece in near + far]
    return difference(place, high, low, kinds[3], twins, model, image, valids)[None]


def solution(mesh):
    placed = (
        P(("patch", "epoch"), None, None),
        P(("patch", "epoch"), None, None),
        P("patch", None, None),
        P("patch"),
    )
    return jax.shard_map(
        part_of_epoch,
        mesh=mesh,
        in_specs=placed,
        out_specs=P(("patch", "epoch"), None, None),
        check_vma=False,
    )
```

```python
import functools
import math

import jax
import jax.numpy as jnp
import numpy as np
from jax import lax
from jax.experimental import pallas as pl
from jax.experimental.pallas import tpu as pltpu
from jax.sharding import PartitionSpec as P

HALF = 15
MARGIN = 16
LANES = 128
SHIFTS = 8
GROUPS = 4
GRANT = 12 << 20
STREAMS = 2
PRODUCT = 1280

gauss_widths = (1.5, 3.0, 6.0)
gauss_degrees = (6, 4, 2)


def basis_filters():
    offsets = np.arange(-HALF, HALF + 1).astype(np.float64)
    result = []
    for width, degree in zip(gauss_widths, gauss_degrees):
        envelope = np.exp(-offsets * offsets / (2.0 * width * width)) / (math.sqrt(2.0 * math.pi) * width)
        for power in range(degree + 1):
            result.append(envelope * (offsets / width) ** power)
    return np.stack(result)


def kernel_pairs():
    result = []
    first_index = 0
    for degree in gauss_degrees:
        for vert_power in range(degree + 1):
            for horiz_power in range(degree + 1 - vert_power):
                result.append((first_index + vert_power, first_index + horiz_power))
        first_index = first_index + degree + 1
    return result


def tables(rows, padded_rows):
    filters = basis_filters()
    count, taps = filters.shape
    pairs = kernel_pairs()
    vert_pick = np.zeros((count + 1, len(pairs)), np.float32)
    horiz_pick = np.zeros((len(pairs), count + 1), np.float32)
    for index, (vert, horiz) in enumerate(pairs):
        vert_pick[vert, index] = 1.0
        horiz_pick[index, horiz] = 1.0
    span = SHIFTS * GROUPS
    horiz = np.zeros((count + 1, span), np.float64)
    horiz[:count, :taps] = filters
    horiz_lanes = np.repeat(horiz, padded_rows, axis=1).astype(np.float32)
    vert = np.zeros((count, rows, padded_rows), np.float64)
    for row in range(rows):
        start = row + MARGIN - HALF
        vert[:, row, start : start + taps] = filters
    vert_lanes = np.tile(vert, (1, 1, LANES // padded_rows)).astype(np.float32)
    return vert_pick, horiz_pick, horiz_lanes, vert_lanes


def mask_kernel(twin, stream, place_ref, octets_ref, image_ref, masked_ref, valid_ref):
    width = masked_ref.shape[1]
    word_count, piece_words = octets_ref.shape[1], width // 32
    piece = ((place_ref[0] & 1) ^ twin) * STREAMS + stream
    word_row = lax.broadcasted_iota(jnp.int32, (piece_words, width), 0)
    lane = lax.broadcasted_iota(jnp.int32, (piece_words, width), 1)
    spread = jnp.where(word_row == jnp.right_shift(lane, 5), 1.0, 0.0).astype(jnp.bfloat16)
    octets = pltpu.roll(octets_ref[...], lax.rem(word_count - piece * piece_words, word_count), 1)
    octets = octets[:, :piece_words].astype(jnp.bfloat16)
    wide = jnp.dot(octets, spread, preferred_element_type=jnp.float32).astype(jnp.int32)
    lane = lax.broadcasted_iota(jnp.int32, wide.shape, 1)
    byte_row = lax.broadcasted_iota(jnp.int32, wide.shape, 0)
    bit = jnp.right_shift(wide, lane & 7) & 1
    bit = jnp.where(byte_row == (jnp.right_shift(lane, 3) & 3), bit, 0).astype(jnp.float32)
    valid = jnp.sum(bit, axis=0, keepdims=True)
    valid_ref[...] = valid
    row = lax.broadcasted_iota(jnp.int32, masked_ref.shape, 0)
    cells = image_ref[:, pl.ds(pl.multiple_of(piece * width, width), width)]
    masked_ref[...] = jnp.where(row == 0, valid, valid * cells)


def masked_piece(place, octets, image, twin, stream):
    rows, columns = image.shape
    width = columns // (2 * STREAMS)
    vmem = pl.BlockSpec(memory_space=pltpu.VMEM)
    return pl.pallas_call(
        functools.partial(mask_kernel, twin, stream),
        in_specs=[pl.BlockSpec(memory_space=pltpu.SMEM), vmem, vmem],
        out_specs=[vmem, vmem],
        out_shape=[
            jax.ShapeDtypeStruct((rows, width), jnp.float32),
            jax.ShapeDtypeStruct((1, width), jnp.float32),
        ],
        compiler_params=pltpu.CompilerParams(vmem_limit_bytes=GRANT),
        cost_estimate=pl.CostEstimate(flops=rows * width, bytes_accessed=8 * rows * width, transcendentals=0),
        name="mask_piece",
    )(place, octets, image)


def part_kernel(bit, place_ref, kept_ref, arrived_ref, keep_ref, send_ref):
    width = keep_ref.shape[1]
    side = jnp.right_shift(place_ref[0], bit) & 1
    for target_ref, part in ((keep_ref, side), (send_ref, 1 - side)):
        lanes = pl.ds(pl.multiple_of(part * width, width), width)
        target_ref[...] = kept_ref[:, lanes] + arrived_ref[:, lanes]


def add_and_part(place, bit, kept, arrived):
    rows, width = kept.shape
    if width % (2 * LANES):
        return halves(kept + arrived, jnp.right_shift(place[0], bit) & 1)
    vmem = pl.BlockSpec(memory_space=pltpu.VMEM)
    return pl.pallas_call(
        functools.partial(part_kernel, bit),
        in_specs=[pl.BlockSpec(memory_space=pltpu.SMEM), vmem, vmem],
        out_specs=[vmem, vmem],
        out_shape=[jax.ShapeDtypeStruct((rows, width // 2), jnp.float32)] * 2,
        compiler_params=pltpu.CompilerParams(vmem_limit_bytes=GRANT),
        cost_estimate=pl.CostEstimate(flops=rows * width, bytes_accessed=12 * rows * width, transcendentals=0),
        name="add_and_part",
    )(place, kept, arrived)


def weight_kernel(place_ref, order_ref, coef_ref, vert_pick_ref, horiz_pick_ref, horiz_ref, vert_ref, high_ref, low_ref):
    count, rows, lanes = vert_ref.shape
    exact = dict(precision=lax.Precision.HIGHEST, preferred_element_type=jnp.float32)
    order = order_ref[...]
    slot = lax.broadcasted_iota(jnp.int32, order.shape, 1)
    catalog = jnp.sum(jnp.where(slot == place_ref[0], order, 0), axis=1, keepdims=True)
    chosen = lax.broadcasted_iota(jnp.int32, coef_ref.shape[1:], 0) == catalog
    picked = [
        vert_pick_ref[...] * jnp.sum(jnp.where(chosen, coef_ref[term], 0.0), axis=0, keepdims=True)
        for term in range(3)
    ]
    table = jnp.dot(jnp.concatenate(picked, axis=0), horiz_pick_ref[...], **exact)
    taps = jnp.dot(table, horiz_ref[...], **exact)
    step = count + 1
    row = lax.broadcasted_iota(jnp.int32, (rows, lanes), 0).astype(jnp.float32)
    row_pos = (2.0 * row + 1.0) / rows - 1.0
    width = high_ref.shape[1]
    for group in range(GROUPS):
        for start in range(0, width, lanes):
            sums = []
            for term in range(3):
                total = jnp.zeros((rows, lanes), jnp.float32)
                for index in range(count):
                    line = term * step + index
                    first = group * width + start
                    total = total + taps[line : line + 1, first : first + lanes] * vert_ref[index]
                sums.append(total)
            for place, weight in enumerate((sums[0] + row_pos * sums[2], sums[1])):
                high = weight.astype(jnp.bfloat16)
                low = (weight - high.astype(jnp.float32)).astype(jnp.bfloat16)
                first = (2 * group + place) * rows
                high_ref[first : first + rows, start : start + lanes] = high
                low_ref[first : first + rows, start : start + lanes] = low


def weights(place, coefficients, epoch_order, rows, padded_rows):
    arrays = (epoch_order[None], jnp.transpose(coefficients, (2, 0, 1)),) + tables(rows, padded_rows)
    shape = (2 * GROUPS * rows, SHIFTS * padded_rows)
    smem = pl.BlockSpec(memory_space=pltpu.SMEM)
    vmem = pl.BlockSpec(memory_space=pltpu.VMEM)
    return pl.pallas_call(
        weight_kernel,
        in_specs=[smem] + [vmem] * len(arrays),
        out_specs=[vmem, vmem],
        out_shape=[jax.ShapeDtypeStruct(shape, jnp.bfloat16)] * 2,
        compiler_params=pltpu.CompilerParams(vmem_limit_bytes=GRANT),
        cost_estimate=pl.CostEstimate(flops=10**8, bytes_accessed=2 * 10**6, transcendentals=0),
        name="kernel_weights",
    )(place, *arrays)


def widen(template, lanes, wide_high, wide_low):
    padded_rows, columns = template.shape
    domain = columns + LANES
    template = jnp.concatenate([template, jnp.zeros((padded_rows, LANES), jnp.float32)], axis=1)
    for shift in range(SHIFTS):
        moved = template if shift == 0 else pltpu.roll(template, domain - shift, 1)
        high = moved.astype(jnp.bfloat16)
        low = (moved - high.astype(jnp.float32)).astype(jnp.bfloat16)
        wide_high[shift * padded_rows : (shift + 1) * padded_rows, lanes] = high
        wide_low[shift * padded_rows : (shift + 1) * padded_rows, lanes] = low


def multiply(high_ref, low_ref, wide_high, wide_low, partial):
    lanes = partial.shape[1]
    block = PRODUCT if lanes % PRODUCT == 0 else lanes
    for start in range(0, lanes, block):
        here = slice(start, start + block)
        high = wide_high[:, here]
        total = jnp.dot(high_ref[...], high, preferred_element_type=jnp.float32)
        total += jnp.dot(low_ref[...], high, preferred_element_type=jnp.float32)
        total += jnp.dot(high_ref[...], wide_low[:, here], preferred_element_type=jnp.float32)
        partial[:, here] = total


def gathered(partial, lanes, first_column, total_columns):
    size = partial.shape[0] // GROUPS
    rows = size // 2
    domain = lanes.stop - lanes.start
    total = jnp.zeros((size, domain), jnp.float32)
    for group in range(GROUPS):
        amount = (HALF - SHIFTS * group) % domain
        total = total + pltpu.roll(partial[group * size : (group + 1) * size, lanes], amount, 1)
    lane = lax.broadcasted_iota(jnp.int32, (rows, domain), 1)
    column = first_column + jnp.where(lane < domain - LANES // 2, lane, lane - domain)
    position = (2.0 * column.astype(jnp.float32) + 1.0) / total_columns - 1.0
    return total[:rows] + position * total[rows:]


def piece_column(place, twin, stream, choices, half):
    width = half // STREAMS
    first = ((place & 1) ^ twin) * half + stream * width
    for bit, other in choices:
        width = width // 2
        first = first + ((jnp.right_shift(place, bit) & 1) ^ other) * width
    return pl.multiple_of(first, LANES)


def add_pieces(pieces, place, high_ref, low_ref, template_refs, total_columns, model_ref, scratch):
    wide_high, wide_low, partial = scratch
    lane = lax.broadcasted_iota(jnp.int32, (model_ref.shape[0], LANES), 1)
    spans, stop = [], 0
    for template_ref in template_refs:
        start, stop = stop, stop + template_ref.shape[1] + LANES
        spans.append(slice(start, stop))
    for span, template_ref in zip(spans, template_refs):
        widen(template_ref[...], span, wide_high, wide_low)
    multiply(high_ref, low_ref, wide_high, wide_low, partial)
    for span, piece in zip(spans, pieces):
        width = span.stop - span.start - LANES
        first = piece_column(place, *piece, total_columns // 2)
        model = gathered(partial, span, first, total_columns)
        spill = model[:, width:]
        body = pl.ds(pl.multiple_of(first + LANES, LANES), width)
        model_ref[:, body] = model_ref[:, body] + model[:, :width]
        before = pl.ds(first, LANES)
        model_ref[:, before] = model_ref[:, before] + jnp.where(lane < LANES // 2, 0.0, spill)
        after = pl.ds(pl.multiple_of(first + (LANES + width), LANES), LANES)
        model_ref[:, after] = model_ref[:, after] + jnp.where(lane < LANES // 2, spill, 0.0)


def model_kernel(pieces, total_columns, fresh, place_ref, high_ref, low_ref, *refs):
    count = len(pieces)
    templates, refs = refs[:count], refs[count:]
    if fresh:
        model_ref, scratch = refs[0], refs[1:]
        model_ref[...] = jnp.zeros_like(model_ref)
    else:
        model_ref, scratch = refs[1], refs[2:]
    add_pieces(pieces, place_ref[0], high_ref, low_ref, templates, total_columns, model_ref, scratch)


def difference_kernel(pieces, place_ref, high_ref, low_ref, *refs):
    count, parts = len(pieces), 2 * STREAMS
    templates, refs = refs[:count], refs[count:]
    model_ref, image_ref, valid_refs = refs[0], refs[1], refs[2 : 2 + parts]
    out_ref, total_ref, valid_all, ready, early_sem, late_sem = refs[2 + parts : 8 + parts]
    rows, columns = out_ref.shape
    half, width = columns // 2, columns // parts
    side = place_ref[0] & 1
    for part, valid_ref in enumerate(valid_refs):
        first = ((side ^ (part // STREAMS)) * STREAMS + part % STREAMS) * width
        valid_all[:, pl.ds(pl.multiple_of(first, width), width)] = valid_ref[...]

    def finish(first, size, model, sem):
        first = pl.multiple_of(first, LANES)
        lanes = pl.ds(first, size)
        centre = image_ref[MARGIN : MARGIN + rows, lanes]
        ready[:, lanes] = valid_all[:, lanes] * (centre - model[:, pl.ds(pl.multiple_of(first + LANES, LANES), size)])
        copy = pltpu.make_async_copy(ready.at[:, lanes], out_ref.at[:, lanes], sem)
        copy.start()
        return copy

    early = finish(side * (half + LANES), half - LANES, model_ref, early_sem)
    total_ref[...] = model_ref[...]
    add_pieces(pieces, place_ref[0], high_ref, low_ref, templates, columns, total_ref, refs[8 + parts :])
    late = finish((1 - side) * (half - LANES), half + LANES, total_ref, late_sem)
    early.wait()
    late.wait()


def model_scratch(rows, templates):
    padded_rows = templates[0].shape[0]
    lanes = sum(template.shape[1] + LANES for template in templates)
    return [
        pltpu.VMEM((SHIFTS * padded_rows, lanes), jnp.bfloat16),
        pltpu.VMEM((SHIFTS * padded_rows, lanes), jnp.bfloat16),
        pltpu.VMEM((2 * GROUPS * rows, lanes), jnp.float32),
    ]


def model_cost(rows, templates):
    padded_rows = templates[0].shape[0]
    lanes = sum(template.shape[1] + LANES for template in templates)
    flops = 12 * GROUPS * rows * SHIFTS * padded_rows * lanes
    return pl.CostEstimate(flops=flops, bytes_accessed=10 * padded_rows * lanes, transcendentals=0)


def norm_kernel(kept_ref, arrived_ref, out_ref):
    total = kept_ref[...] + arrived_ref[...]
    out_ref[...] = total / jnp.maximum(total[:1], 1.0)


def template_of(kept, arrived):
    vmem = pl.BlockSpec(memory_space=pltpu.VMEM)
    return pl.pallas_call(
        norm_kernel,
        in_specs=[vmem, vmem],
        out_specs=vmem,
        out_shape=jax.ShapeDtypeStruct(kept.shape, jnp.float32),
        compiler_params=pltpu.CompilerParams(vmem_limit_bytes=GRANT),
        cost_estimate=pl.CostEstimate(flops=4 * kept.size, bytes_accessed=12 * kept.size, transcendentals=0),
        name="template",
    )(kept, arrived)


def add_models(place, high, low, pieces, templates, model, rows, total_columns):
    count = len(templates)
    fresh = model is None
    vmem = pl.BlockSpec(memory_space=pltpu.VMEM)
    return pl.pallas_call(
        functools.partial(model_kernel, pieces, total_columns, fresh),
        in_specs=[pl.BlockSpec(memory_space=pltpu.SMEM)] + [vmem] * (2 + count + (not fresh)),
        out_specs=vmem,
        out_shape=jax.ShapeDtypeStruct((rows, total_columns + 2 * LANES), jnp.float32),
        scratch_shapes=model_scratch(rows, templates),
        input_output_aliases={} if fresh else {3 + count: 0},
        compiler_params=pltpu.CompilerParams(vmem_limit_bytes=GRANT),
        cost_estimate=model_cost(rows, templates),
        name="add_models",
    )(place, high, low, *templates, *(() if fresh else (model,)))


def difference(place, high, low, pieces, templates, model, image, valids):
    rows, columns = model.shape[0], image.shape[1]
    vmem = pl.BlockSpec(memory_space=pltpu.VMEM)
    return pl.pallas_call(
        functools.partial(difference_kernel, pieces),
        in_specs=[pl.BlockSpec(memory_space=pltpu.SMEM)] + [vmem] * (4 + len(templates) + len(valids)),
        out_specs=pl.BlockSpec(memory_space=pl.ANY),
        out_shape=jax.ShapeDtypeStruct((rows, columns), jnp.float32),
        scratch_shapes=[
            pltpu.VMEM(model.shape, jnp.float32),
            pltpu.VMEM((1, columns), jnp.float32),
            pltpu.VMEM((rows, columns), jnp.float32),
            pltpu.SemaphoreType.DMA,
            pltpu.SemaphoreType.DMA,
        ]
        + model_scratch(rows, templates),
        compiler_params=pltpu.CompilerParams(vmem_limit_bytes=GRANT),
        cost_estimate=model_cost(rows, templates),
        name="difference",
    )(place, high, low, *templates, model, image, *valids)


def exchange(cells, bit):
    count = lax.axis_size("epoch")
    return lax.ppermute(cells, "epoch", [(i, i ^ (1 << bit)) for i in range(count)])


def halves(cells, side):
    width = cells.shape[1] // 2
    keep = lax.dynamic_slice_in_dim(cells, side * width, width, 1)
    send = lax.dynamic_slice_in_dim(cells, (1 - side) * width, width, 1)
    return keep, send


def joined_columns(cells, other, side):
    return jnp.where(side == 0, jnp.concatenate([cells, other], axis=1), jnp.concatenate([other, cells], axis=1))


def part_of_epoch(epoch_images, mask_words, coefficients, epoch_order):
    padded_rows, columns = epoch_images.shape[1:]
    rows = padded_rows - 2 * MARGIN
    index = lax.axis_index("epoch").astype(jnp.int32)
    place = index[None]
    bits = lax.axis_size("epoch").bit_length() - 1
    image, words = epoch_images[0], mask_words[0]
    orders = list(range(1, bits - 1)), [2, 1] + list(range(3, bits - 1))
    streams = range(STREAMS)

    places = 8 * (lax.broadcasted_iota(jnp.int32, (8, words.shape[1]), 0) & 3)
    octets = (jnp.right_shift(jnp.broadcast_to(words, places.shape), places) & 255).astype(jnp.float32)
    far, near = [], []
    for stream in streams:
        far.append(masked_piece(place, octets, image, 1, stream))
    others = [exchange(far[stream][0], 0) for stream in streams]
    for stream in streams:
        near.append(masked_piece(place, octets, image, 0, stream))
    cells = [near[stream][0] for stream in streams]
    for step in range(bits - 2):
        pairs = [add_and_part(place, orders[stream][step], cells[stream], others[stream]) for stream in streams]
        cells = [pairs[stream][0] for stream in streams]
        others = [exchange(pairs[stream][1], orders[stream][step]) for stream in streams]
    cells = [cells[stream] + others[stream] for stream in streams]
    others = [exchange(cells[stream], bits - 1) for stream in streams]
    high, low = weights(place, coefficients, epoch_order, rows, padded_rows)
    for stream in streams:
        cells[stream] = template_of(cells[stream], others[stream])

    def joined(cells, others, step):
        return [
            joined_columns(cells[stream], others[stream], jnp.right_shift(index, orders[stream][step]) & 1)
            for stream in streams
        ]

    def gather_step(cells, step):
        return [exchange(cells[stream], orders[stream][step]) for stream in streams]

    def pieces(twin, others):
        return [
            (twin, stream, tuple((orders[stream][level], other) for level, other in enumerate(others)))
            for stream in streams
        ]

    for step in reversed(range(2, bits - 2)):
        cells = joined(cells, gather_step(cells, step), step)
    others = gather_step(cells, 1)
    twins = [exchange(cells[stream], 0) for stream in streams]
    model = add_models(place, high, low, pieces(0, (0, 0)), cells, None, rows, columns)
    cells, quarter = joined(cells, others, 1), others
    others = gather_step(cells, 0)
    model = add_models(place, high, low, pieces(0, (0, 1)) + pieces(1, (0, 0)), quarter + twins, model, rows, columns)
    twins = [exchange(quarter[stream], 0) for stream in streams]
    ends = [exchange(others[stream], 0) for stream in streams]
    model = add_models(place, high, low, pieces(1, (0, 1)), twins, model, rows, columns)
    model = add_models(place, high, low, pieces(0, (1,)), others, model, rows, columns)
    valids = [piece[1] for piece in near + far]
    return difference(place, high, low, pieces(1, (1,)), ends, model, image, valids)[None]


def solution(mesh):
    placed = (
        P(("patch", "epoch"), None, None),
        P(("patch", "epoch"), None, None),
        P("patch", None, None),
        P("patch"),
    )
    return jax.shard_map(
        part_of_epoch,
        mesh=mesh,
        in_specs=placed,
        out_specs=P(("patch", "epoch"), None, None),
        check_vma=False,
    )
```

```python
import functools
import math

import jax
import jax.numpy as jnp
import numpy as np
from jax import lax
from jax.experimental import pallas as pl
from jax.experimental.pallas import tpu as pltpu
from jax.sharding import PartitionSpec as P

HALF = 15
MARGIN = 16
LANES = 128
SHIFTS = 8
GROUPS = 4
GRANT = 12 << 20
FULL_GRANT = 67043328 - (2000 << 10)
STREAMS = 2
PRODUCT = 256

gauss_widths = (1.5, 3.0, 6.0)
gauss_degrees = (6, 4, 2)


def basis_filters():
    offsets = np.arange(-HALF, HALF + 1).astype(np.float64)
    result = []
    for width, degree in zip(gauss_widths, gauss_degrees):
        envelope = np.exp(-offsets * offsets / (2.0 * width * width)) / (math.sqrt(2.0 * math.pi) * width)
        for power in range(degree + 1):
            result.append(envelope * (offsets / width) ** power)
    return np.stack(result)


def kernel_pairs():
    result = []
    first_index = 0
    for degree in gauss_degrees:
        for vert_power in range(degree + 1):
            for horiz_power in range(degree + 1 - vert_power):
                result.append((first_index + vert_power, first_index + horiz_power))
        first_index = first_index + degree + 1
    return result


def tables(rows, padded_rows):
    filters = basis_filters()
    count, taps = filters.shape
    pairs = kernel_pairs()
    vert_pick = np.zeros((count + 1, len(pairs)), np.float32)
    horiz_pick = np.zeros((len(pairs), count + 1), np.float32)
    for index, (vert, horiz) in enumerate(pairs):
        vert_pick[vert, index] = 1.0
        horiz_pick[index, horiz] = 1.0
    span = SHIFTS * GROUPS
    horiz = np.zeros((count + 1, span), np.float64)
    horiz[:count, :taps] = filters
    horiz_lanes = np.repeat(horiz, padded_rows, axis=1).astype(np.float32)
    vert = np.zeros((count, rows, padded_rows), np.float64)
    for row in range(rows):
        start = row + MARGIN - HALF
        vert[:, row, start : start + taps] = filters
    vert_lanes = np.tile(vert, (1, 1, LANES // padded_rows)).astype(np.float32)
    return vert_pick, horiz_pick, horiz_lanes, vert_lanes


def octets_of(words):
    byte_row = lax.broadcasted_iota(jnp.int32, (8, words.shape[1]), 0)
    octets = jnp.right_shift(jnp.broadcast_to(words, byte_row.shape), 8 * (byte_row & 3)) & 255
    return octets.astype(jnp.float32)


def valid_lanes(octets, piece, width):
    word_count, piece_words = octets.shape[1], width // 32
    word_row = lax.broadcasted_iota(jnp.int32, (piece_words, width), 0)
    lane = lax.broadcasted_iota(jnp.int32, (piece_words, width), 1)
    spread = jnp.where(word_row == jnp.right_shift(lane, 5), 1.0, 0.0).astype(jnp.bfloat16)
    octets = pltpu.roll(octets, lax.rem(word_count - piece * piece_words, word_count), 1)
    octets = octets[:, :piece_words].astype(jnp.bfloat16)
    wide = jnp.dot(octets, spread, preferred_element_type=jnp.float32).astype(jnp.int32)
    lane = lax.broadcasted_iota(jnp.int32, wide.shape, 1)
    byte_row = lax.broadcasted_iota(jnp.int32, wide.shape, 0)
    bit = jnp.right_shift(wide, lane & 7) & 1
    bit = jnp.where(byte_row == (jnp.right_shift(lane, 3) & 3), bit, 0).astype(jnp.float32)
    return jnp.sum(bit, axis=0, keepdims=True)


def masked(valid, cells):
    row = lax.broadcasted_iota(jnp.int32, cells.shape, 0)
    return jnp.where(row == 0, valid, valid * cells)


def first_kernel(stream, place_ref, words_ref, image_ref, masked_ref, words, cells, word_sem, cell_sem):
    width = cells.shape[1]
    piece = (1 - (place_ref[0] & 1)) * STREAMS + stream
    lanes = pl.ds(pl.multiple_of(piece * width, width), width)
    copies = (
        pltpu.make_async_copy(words_ref, words, word_sem),
        pltpu.make_async_copy(image_ref.at[:, lanes], cells, cell_sem),
    )
    for copy in copies:
        copy.start()
    copies[0].wait()
    valid = valid_lanes(octets_of(words[...]), piece, width)
    copies[1].wait()
    masked_ref[...] = masked(valid, cells[...])


def first_piece(place, words, image, stream):
    rows, columns = image.shape
    width = columns // (2 * STREAMS)
    anywhere = pl.BlockSpec(memory_space=pl.ANY)
    return pl.pallas_call(
        functools.partial(first_kernel, stream),
        in_specs=[pl.BlockSpec(memory_space=pltpu.SMEM), anywhere, anywhere],
        out_specs=pl.BlockSpec(memory_space=pltpu.VMEM),
        out_shape=jax.ShapeDtypeStruct((rows, width), jnp.float32),
        scratch_shapes=[
            pltpu.VMEM(words.shape, jnp.int32),
            pltpu.VMEM((rows, width), jnp.float32),
            pltpu.SemaphoreType.DMA,
            pltpu.SemaphoreType.DMA,
        ],
        compiler_params=pltpu.CompilerParams(vmem_limit_bytes=FULL_GRANT),
        cost_estimate=pl.CostEstimate(flops=rows * width, bytes_accessed=8 * rows * width, transcendentals=0),
        name="first_piece",
    )(place, words, image)


def mask_kernel(twin, stream, place_ref, words_ref, image_ref, masked_ref, *valid_refs):
    width = masked_ref.shape[1]
    octets = octets_of(words_ref[...])
    base = ((place_ref[0] & 1) ^ twin) * STREAMS
    for index, valid_ref in enumerate(valid_refs):
        valid_ref[...] = valid_lanes(octets, base + (stream + index) % STREAMS, width)
    lanes = pl.ds(pl.multiple_of((base + stream) * width, width), width)
    masked_ref[...] = masked(valid_refs[0][...], image_ref[:, lanes])


def masked_piece(place, words, image, twin, stream, valids):
    rows, columns = image.shape
    width = columns // (2 * STREAMS)
    vmem = pl.BlockSpec(memory_space=pltpu.VMEM)
    return pl.pallas_call(
        functools.partial(mask_kernel, twin, stream),
        in_specs=[pl.BlockSpec(memory_space=pltpu.SMEM), vmem, vmem],
        out_specs=[vmem] * (1 + valids),
        out_shape=[jax.ShapeDtypeStruct((rows, width), jnp.float32)]
        + [jax.ShapeDtypeStruct((1, width), jnp.float32)] * valids,
        compiler_params=pltpu.CompilerParams(vmem_limit_bytes=GRANT),
        cost_estimate=pl.CostEstimate(flops=rows * width, bytes_accessed=8 * rows * width, transcendentals=0),
        name="mask_piece",
    )(place, words, image)


def part_kernel(bit, place_ref, kept_ref, arrived_ref, keep_ref, send_ref):
    width = keep_ref.shape[1]
    side = jnp.right_shift(place_ref[0], bit) & 1
    for target_ref, part in ((keep_ref, side), (send_ref, 1 - side)):
        lanes = pl.ds(pl.multiple_of(part * width, width), width)
        target_ref[...] = kept_ref[:, lanes] + arrived_ref[:, lanes]


def add_and_part(place, bit, kept, arrived):
    rows, width = kept.shape
    if width % (2 * LANES):
        return halves(kept + arrived, jnp.right_shift(place[0], bit) & 1)
    vmem = pl.BlockSpec(memory_space=pltpu.VMEM)
    return pl.pallas_call(
        functools.partial(part_kernel, bit),
        in_specs=[pl.BlockSpec(memory_space=pltpu.SMEM), vmem, vmem],
        out_specs=[vmem, vmem],
        out_shape=[jax.ShapeDtypeStruct((rows, width // 2), jnp.float32)] * 2,
        compiler_params=pltpu.CompilerParams(vmem_limit_bytes=GRANT),
        cost_estimate=pl.CostEstimate(flops=rows * width, bytes_accessed=12 * rows * width, transcendentals=0),
        name="add_and_part",
    )(place, kept, arrived)


def weight_kernel(place_ref, order_ref, coef_ref, vert_pick_ref, horiz_pick_ref, horiz_ref, vert_ref, high_ref, low_ref):
    count, rows, lanes = vert_ref.shape
    exact = dict(precision=lax.Precision.HIGHEST, preferred_element_type=jnp.float32)
    order = order_ref[...]
    slot = lax.broadcasted_iota(jnp.int32, order.shape, 1)
    catalog = jnp.sum(jnp.where(slot == place_ref[0], order, 0), axis=1, keepdims=True)
    chosen = lax.broadcasted_iota(jnp.int32, coef_ref.shape[1:], 0) == catalog
    picked = [
        vert_pick_ref[...] * jnp.sum(jnp.where(chosen, coef_ref[term], 0.0), axis=0, keepdims=True)
        for term in range(3)
    ]
    table = jnp.dot(jnp.concatenate(picked, axis=0), horiz_pick_ref[...], **exact)
    taps = jnp.dot(table, horiz_ref[...], **exact)
    step = count + 1
    row = lax.broadcasted_iota(jnp.int32, (rows, lanes), 0).astype(jnp.float32)
    row_pos = (2.0 * row + 1.0) / rows - 1.0
    width = high_ref.shape[1]
    for group in range(GROUPS):
        for start in range(0, width, lanes):
            sums = []
            for term in range(3):
                total = jnp.zeros((rows, lanes), jnp.float32)
                for index in range(count):
                    line = term * step + index
                    first = group * width + start
                    total = total + taps[line : line + 1, first : first + lanes] * vert_ref[index]
                sums.append(total)
            for place, weight in enumerate((sums[0] + row_pos * sums[2], sums[1])):
                high = weight.astype(jnp.bfloat16)
                low = (weight - high.astype(jnp.float32)).astype(jnp.bfloat16)
                first = (2 * group + place) * rows
                high_ref[first : first + rows, start : start + lanes] = high
                low_ref[first : first + rows, start : start + lanes] = low


def weights(place, coefficients, epoch_order, rows, padded_rows):
    arrays = (epoch_order[None], jnp.transpose(coefficients, (2, 0, 1)),) + tables(rows, padded_rows)
    shape = (2 * GROUPS * rows, SHIFTS * padded_rows)
    smem = pl.BlockSpec(memory_space=pltpu.SMEM)
    vmem = pl.BlockSpec(memory_space=pltpu.VMEM)
    return pl.pallas_call(
        weight_kernel,
        in_specs=[smem] + [vmem] * len(arrays),
        out_specs=[vmem, vmem],
        out_shape=[jax.ShapeDtypeStruct(shape, jnp.bfloat16)] * 2,
        compiler_params=pltpu.CompilerParams(vmem_limit_bytes=GRANT),
        cost_estimate=pl.CostEstimate(flops=10**8, bytes_accessed=2 * 10**6, transcendentals=0),
        name="kernel_weights",
    )(place, *arrays)


def widen(template, lanes, wide_high, wide_low):
    padded_rows, columns = template.shape
    domain = columns + LANES
    template = jnp.concatenate([template, jnp.zeros((padded_rows, LANES), jnp.float32)], axis=1)
    main = template.astype(jnp.bfloat16).astype(jnp.float32)
    for wide, part in ((wide_high, main), (wide_low, template - main)):
        for shift in range(SHIFTS):
            moved = part if shift == 0 else pltpu.roll(part, domain - shift, 1)
            wide[shift * padded_rows : (shift + 1) * padded_rows, lanes] = moved.astype(jnp.bfloat16)


def multiply(high_ref, low_ref, wide_high, wide_low, partial):
    lanes = partial.shape[1]
    for start in range(0, lanes, PRODUCT):
        here = slice(start, min(start + PRODUCT, lanes))
        high = wide_high[:, here]
        total = jnp.dot(high_ref[...], high, preferred_element_type=jnp.float32)
        total += jnp.dot(low_ref[...], high, preferred_element_type=jnp.float32)
        total += jnp.dot(high_ref[...], wide_low[:, here], preferred_element_type=jnp.float32)
        partial[:, here] = total


def gathered(partial, lanes, first_column, total_columns):
    size = partial.shape[0] // GROUPS
    rows = size // 2
    domain = lanes.stop - lanes.start
    total = jnp.zeros((size, domain), jnp.float32)
    for group in range(GROUPS):
        amount = (HALF - SHIFTS * group) % domain
        total = total + pltpu.roll(partial[group * size : (group + 1) * size, lanes], amount, 1)
    lane = lax.broadcasted_iota(jnp.int32, (rows, domain), 1)
    column = first_column + jnp.where(lane < domain - LANES // 2, lane, lane - domain)
    position = (2.0 * column.astype(jnp.float32) + 1.0) / total_columns - 1.0
    return total[:rows] + position * total[rows:]


def piece_column(place, twin, stream, choices, half):
    width = half // STREAMS
    first = ((place & 1) ^ twin) * half + stream * width
    for bit, other in choices:
        width = width // 2
        first = first + ((jnp.right_shift(place, bit) & 1) ^ other) * width
    return pl.multiple_of(first, LANES)


def add_pieces(pieces, place, high_ref, low_ref, template_refs, total_columns, model_ref, scratch):
    wide_high, wide_low, partial = scratch
    lane = lax.broadcasted_iota(jnp.int32, (model_ref.shape[0], LANES), 1)
    spans, stop = [], 0
    for template_ref in template_refs:
        start, stop = stop, stop + template_ref.shape[1] + LANES
        spans.append(slice(start, stop))
    for span, template_ref in zip(spans, template_refs):
        widen(template_ref[...], span, wide_high, wide_low)
    multiply(high_ref, low_ref, wide_high, wide_low, partial)
    for span, piece in zip(spans, pieces):
        width = span.stop - span.start - LANES
        first = piece_column(place, *piece, total_columns // 2)
        model = gathered(partial, span, first, total_columns)
        spill = model[:, width:]
        body = pl.ds(pl.multiple_of(first + LANES, LANES), width)
        model_ref[:, body] = model_ref[:, body] + model[:, :width]
        before = pl.ds(first, LANES)
        model_ref[:, before] = model_ref[:, before] + jnp.where(lane < LANES // 2, 0.0, spill)
        after = pl.ds(pl.multiple_of(first + (LANES + width), LANES), LANES)
        model_ref[:, after] = model_ref[:, after] + jnp.where(lane < LANES // 2, spill, 0.0)


def model_kernel(pieces, total_columns, fresh, place_ref, high_ref, low_ref, *refs):
    count = len(pieces)
    templates, refs = refs[:count], refs[count:]
    if fresh:
        model_ref, scratch = refs[0], refs[1:]
        model_ref[...] = jnp.zeros_like(model_ref)
    else:
        model_ref, scratch = refs[1], refs[2:]
    add_pieces(pieces, place_ref[0], high_ref, low_ref, templates, total_columns, model_ref, scratch)


def difference_kernel(pieces, place_ref, high_ref, low_ref, *refs):
    count, parts = len(pieces), 2 * STREAMS
    templates, refs = refs[:count], refs[count:]
    model_ref, image_ref, valid_refs = refs[0], refs[1], refs[2 : 2 + parts]
    out_ref, total_ref, valid_all, ready, early_sem, late_sem = refs[2 + parts : 8 + parts]
    rows, columns = out_ref.shape
    half, width = columns // 2, columns // parts
    side = place_ref[0] & 1
    for part, valid_ref in enumerate(valid_refs):
        first = ((side ^ (part // STREAMS)) * STREAMS + part % STREAMS) * width
        valid_all[:, pl.ds(pl.multiple_of(first, width), width)] = valid_ref[...]

    def finish(first, size, model, sem):
        first = pl.multiple_of(first, LANES)
        lanes = pl.ds(first, size)
        centre = image_ref[MARGIN : MARGIN + rows, lanes]
        ready[:, lanes] = valid_all[:, lanes] * (centre - model[:, pl.ds(pl.multiple_of(first + LANES, LANES), size)])
        copy = pltpu.make_async_copy(ready.at[:, lanes], out_ref.at[:, lanes], sem)
        copy.start()
        return copy

    early = finish(side * (half + LANES), half - LANES, model_ref, early_sem)
    total_ref[...] = model_ref[...]
    add_pieces(pieces, place_ref[0], high_ref, low_ref, templates, columns, total_ref, refs[8 + parts :])
    late = finish((1 - side) * (half - LANES), half + LANES, total_ref, late_sem)
    early.wait()
    late.wait()


def model_scratch(rows, templates):
    padded_rows = templates[0].shape[0]
    lanes = sum(template.shape[1] + LANES for template in templates)
    return [
        pltpu.VMEM((SHIFTS * padded_rows, lanes), jnp.bfloat16),
        pltpu.VMEM((SHIFTS * padded_rows, lanes), jnp.bfloat16),
        pltpu.VMEM((2 * GROUPS * rows, lanes), jnp.float32),
    ]


def model_cost(rows, templates):
    padded_rows = templates[0].shape[0]
    lanes = sum(template.shape[1] + LANES for template in templates)
    flops = 12 * GROUPS * rows * SHIFTS * padded_rows * lanes
    return pl.CostEstimate(flops=flops, bytes_accessed=10 * padded_rows * lanes, transcendentals=0)


def norm_kernel(kept_ref, arrived_ref, out_ref):
    total = kept_ref[...] + arrived_ref[...]
    out_ref[...] = total / jnp.maximum(total[:1], 1.0)


def template_of(kept, arrived):
    vmem = pl.BlockSpec(memory_space=pltpu.VMEM)
    return pl.pallas_call(
        norm_kernel,
        in_specs=[vmem, vmem],
        out_specs=vmem,
        out_shape=jax.ShapeDtypeStruct(kept.shape, jnp.float32),
        compiler_params=pltpu.CompilerParams(vmem_limit_bytes=GRANT),
        cost_estimate=pl.CostEstimate(flops=4 * kept.size, bytes_accessed=12 * kept.size, transcendentals=0),
        name="template",
    )(kept, arrived)


def add_models(place, high, low, pieces, templates, model, rows, total_columns):
    count = len(templates)
    fresh = model is None
    vmem = pl.BlockSpec(memory_space=pltpu.VMEM)
    return pl.pallas_call(
        functools.partial(model_kernel, pieces, total_columns, fresh),
        in_specs=[pl.BlockSpec(memory_space=pltpu.SMEM)] + [vmem] * (2 + count + (not fresh)),
        out_specs=vmem,
        out_shape=jax.ShapeDtypeStruct((rows, total_columns + 2 * LANES), jnp.float32),
        scratch_shapes=model_scratch(rows, templates),
        input_output_aliases={} if fresh else {3 + count: 0},
        compiler_params=pltpu.CompilerParams(vmem_limit_bytes=GRANT),
        cost_estimate=model_cost(rows, templates),
        name="add_models",
    )(place, high, low, *templates, *(() if fresh else (model,)))


def difference(place, high, low, pieces, templates, model, image, valids):
    rows, columns = model.shape[0], image.shape[1]
    vmem = pl.BlockSpec(memory_space=pltpu.VMEM)
    return pl.pallas_call(
        functools.partial(difference_kernel, pieces),
        in_specs=[pl.BlockSpec(memory_space=pltpu.SMEM)] + [vmem] * (4 + len(templates) + len(valids)),
        out_specs=pl.BlockSpec(memory_space=pl.ANY),
        out_shape=jax.ShapeDtypeStruct((rows, columns), jnp.float32),
        scratch_shapes=[
            pltpu.VMEM(model.shape, jnp.float32),
            pltpu.VMEM((1, columns), jnp.float32),
            pltpu.VMEM((rows, columns), jnp.float32),
            pltpu.SemaphoreType.DMA,
            pltpu.SemaphoreType.DMA,
        ]
        + model_scratch(rows, templates),
        compiler_params=pltpu.CompilerParams(vmem_limit_bytes=GRANT),
        cost_estimate=model_cost(rows, templates),
        name="difference",
    )(place, high, low, *templates, model, image, *valids)


def exchange(cells, bit):
    count = lax.axis_size("epoch")
    return lax.ppermute(cells, "epoch", [(i, i ^ (1 << bit)) for i in range(count)])


def halves(cells, side):
    width = cells.shape[1] // 2
    keep = lax.dynamic_slice_in_dim(cells, side * width, width, 1)
    send = lax.dynamic_slice_in_dim(cells, (1 - side) * width, width, 1)
    return keep, send


def joined_columns(cells, other, side):
    return jnp.where(side == 0, jnp.concatenate([cells, other], axis=1), jnp.concatenate([other, cells], axis=1))


def part_of_epoch(epoch_images, mask_words, coefficients, epoch_order):
    padded_rows, columns = epoch_images.shape[1:]
    rows = padded_rows - 2 * MARGIN
    index = lax.axis_index("epoch").astype(jnp.int32)
    place = index[None]
    bits = lax.axis_size("epoch").bit_length() - 1
    image, words = epoch_images[0], mask_words[0]
    orders = list(range(1, bits - 1)), [2, 1] + list(range(3, bits - 1))
    streams = range(STREAMS)

    near = []
    sent = first_piece(place, words, image, 1)
    far = masked_piece(place, words, image, 1, 0, 2)
    others = [exchange(cells, 0) for cells in (far[0], sent)]
    for stream in streams:
        near.append(masked_piece(place, words, image, 0, stream, 1))
    cells = [near[stream][0] for stream in streams]
    for step in range(bits - 2):
        pairs = [add_and_part(place, orders[stream][step], cells[stream], others[stream]) for stream in streams]
        cells = [pairs[stream][0] for stream in streams]
        others = [exchange(pairs[stream][1], orders[stream][step]) for stream in streams]
    cells = [cells[stream] + others[stream] for stream in streams]
    others = [exchange(cells[stream], bits - 1) for stream in streams]
    high, low = weights(place, coefficients, epoch_order, rows, padded_rows)
    for stream in streams:
        cells[stream] = template_of(cells[stream], others[stream])

    def joined(cells, others, step):
        return [
            joined_columns(cells[stream], others[stream], jnp.right_shift(index, orders[stream][step]) & 1)
            for stream in streams
        ]

    def gather_step(cells, step):
        return [exchange(cells[stream], orders[stream][step]) for stream in streams]

    def pieces(twin, others):
        return [
            (twin, stream, tuple((orders[stream][level], other) for level, other in enumerate(others)))
            for stream in streams
        ]

    for step in reversed(range(2, bits - 2)):
        cells = joined(cells, gather_step(cells, step), step)
    others = gather_step(cells, 1)
    twins = [exchange(cells[stream], 0) for stream in streams]
    model = add_models(place, high, low, pieces(0, (0, 0)), cells, None, rows, columns)
    cells, quarter = joined(cells, others, 1), others
    others = gather_step(cells, 0)
    model = add_models(place, high, low, pieces(0, (0, 1)) + pieces(1, (0, 0)), quarter + twins, model, rows, columns)
    twins = [exchange(quarter[stream], 0) for stream in streams]
    ends = [exchange(others[stream], 0) for stream in streams]
    model = add_models(place, high, low, pieces(1, (0, 1)), twins, model, rows, columns)
    model = add_models(place, high, low, pieces(0, (1,)), others, model, rows, columns)
    valids = [piece[1] for piece in near] + list(far[1:])
    return difference(place, high, low, pieces(1, (1,)), ends, model, image, valids)[None]


def solution(mesh):
    placed = (
        P(("patch", "epoch"), None, None),
        P(("patch", "epoch"), None, None),
        P("patch", None, None),
        P("patch"),
    )
    return jax.shard_map(
        part_of_epoch,
        mesh=mesh,
        in_specs=placed,
        out_specs=P(("patch", "epoch"), None, None),
        check_vma=False,
    )
```
